32 devices in a mesh: pipe: 4 (over y, x), dp: 8 (over z, core).
Axes of the slice: x: 2, y: 2, z: 4, core: 2. Of those that a mesh axis runs over, the one named last changes fastest.
Arguments:
- cotangent: bfloat16 [4, 1024, 6144], P('pipe', 'dp'), may hold values from -0.29882812 to 0.29882812
- slot_token: int32 [4, 8, 24], P('pipe', 'dp'), may hold values from 0 to 127, as said below
- slot_count: int32 [4, 8], P('pipe', 'dp'), may hold values from 6 to 24, as said below
- slot_weight: float32 [4, 8, 24], P('pipe', 'dp'), may hold values from 0.1 to 0.9
- hidden: bfloat16 [4, 8, 24, 8192], P('pipe', 'dp'), may hold values from -6 to 6
Outputs:
- down_grad: bfloat16 [4, 8192, 6144], P('pipe', 'dp')
The draws below stay inside these ranges and needn't reach their ends.
Inputs may be any that keep to these rules, and one draw needn't show every extreme that they name: `slot_token`: within one device's 24 slots of a section the token indices are distinct. `slot_count`: in every section some device has all 24 slots live.
All inputs are finite; a program needn't handle non-finite values.
Results may differ from the reference program's by a relative error of at most 0.0049.
Values may be sent and summed in bfloat16 or wider, within the bound.
No kernel may reach another device: no remote copies, remote signals or barrier semaphores. Data moves between devices by JAX's collectives and lax.ppermute only.
A program may use at most 128 MiB of HBM per device.

```python
import jax
import jax.numpy as jnp
from jax import lax

D = 6144
HID = 8192
TOK_DEV = 128
CAP = 24
SECTIONS = 4
TOKENS = 1024
N_DP = 8


def draw_slot_token(key, part):
    subkeys = jax.random.split(key, SECTIONS * N_DP)
    chosen = jax.vmap(lambda subkey: jax.random.permutation(subkey, TOK_DEV)[:CAP])(subkeys)
    return chosen.reshape(SECTIONS, N_DP, CAP).astype(jnp.int32)


def draw_slot_count(key, part):
    lowest = max(1, CAP // 4)
    counts = jax.random.randint(jax.random.fold_in(key, 1), (SECTIONS, N_DP), lowest, CAP + 1)
    filled = jax.random.randint(jax.random.fold_in(key, 2), (SECTIONS, 1), 0, N_DP)
    positions = jnp.arange(N_DP, dtype=jnp.int32)[None, :]
    return jnp.where(positions == filled, CAP, counts).astype(jnp.int32)


def shard_levels(key, dims, shards, least, largest):
    loudness, own = 1.0, jax.random.fold_in(key, 6)
    for position, blocks in shards:
        heights = jnp.exp(jax.random.uniform(jax.random.fold_in(own, position), (blocks,), jnp.float32, least / len(shards), largest / len(shards)))
        loudness = loudness * jnp.repeat(heights, dims[position] // blocks).reshape([-1 if axis == position else 1 for axis in range(len(dims))])
    return loudness


def centred(own_key, shape, scale, bound, shards=(), held_as=jnp.bfloat16):
    drawn = jax.random.normal(own_key, shape, jnp.float32) * scale
    if len(shards) > 0:
        drawn = shard_levels(own_key, shape, shards, -0.22, 0.18) * drawn
    return jnp.clip(drawn, min=-bound, max=bound).astype(held_as)


def setup_inputs(seed: int = 0) -> dict:
    key_of = jax.random.split(jax.random.key(seed), 6)
    cotangent = centred(key_of[0], (SECTIONS, TOKENS, D), 0.05, 0.29882812, ((0, 4), (1, 8)))
    slot_token = draw_slot_token(jax.random.fold_in(key_of[5], 71), 0)
    slot_count = draw_slot_count(jax.random.fold_in(key_of[5], 71), 0)
    slot_weight = jnp.clip(0.1 + 0.79999997 * jax.random.uniform(key_of[3], (SECTIONS, N_DP, CAP), jnp.float32) ** shard_levels(key_of[3], (SECTIONS, N_DP, CAP), ((0, 4), (1, 8)), -0.2, 0.2), 0.1, 0.9)
    hidden = centred(key_of[4], (SECTIONS, N_DP, CAP, HID), 1.0, 6.0, ((0, 4), (1, 8)))
    return {"cotangent": cotangent, "slot_token": slot_token, "slot_count": slot_count, "slot_weight": slot_weight, "hidden": hidden}


def reference(cotangent, slot_token, slot_count, slot_weight, hidden):
    upstream = jnp.roll(cotangent, -1, axis=0)

    def one_section(section_data):
        section_up, section_tok, section_cnt, section_wgt, section_hid = section_data
        grouped = section_up.reshape(N_DP, TOK_DEV, D)
        picked = jax.vmap(lambda table, positions: jnp.take(table, positions, axis=0))(grouped, section_tok)
        slot_pos = lax.broadcasted_iota(jnp.int32, (N_DP, CAP), 1)
        live_mask = (slot_pos < section_cnt[:, None]).astype(jnp.float32)
        scaled_rows = ((section_wgt * live_mask)[:, :, None] * picked.astype(jnp.float32)).astype(jnp.bfloat16)
        flat_hidden = section_hid.reshape(N_DP * CAP, HID)
        flat_rows = scaled_rows.reshape(N_DP * CAP, D)
        return jnp.dot(flat_hidden.T, flat_rows, preferred_element_type=jnp.float32).astype(jnp.bfloat16)

    return lax.map(one_section, (upstream, slot_token, slot_count, slot_weight, hidden))
```

```python
import jax
import jax.numpy as jnp
from jax import lax
from jax.experimental import pallas as pl
from jax.experimental.pallas import tpu as pltpu
from jax.sharding import PartitionSpec as P


CORES = 2


def matmul_kernel(half_ref, *refs):
    pieces, ht_ref, out_ref, rows_ref = refs[:-4], refs[-4], refs[-2], refs[-1]
    start = 0
    for piece in pieces:
        rows_ref[start : start + piece.shape[0], :] = piece[...]
        start += piece.shape[0]
    out_ref[...] = jnp.dot(
        ht_ref[...], rows_ref[...], preferred_element_type=jnp.float32
    ).astype(out_ref.dtype)


def matmul_half(half, pieces, ht, out, width):
    hid, slots = ht.shape
    span = width // 2
    tile = 512
    steps = span // tile
    in_specs = [pl.BlockSpec((p.shape[0], tile), lambda i, h: (0, i)) for p in pieces]
    in_specs.append(pl.BlockSpec((hid, slots), lambda i, h: (0, 0)))
    operands = [*pieces, ht]
    in_specs.append(pl.BlockSpec(memory_space=pl.ANY))
    operands.append(out)
    return pl.pallas_call(
        matmul_kernel,
        grid_spec=pltpu.PrefetchScalarGridSpec(
            num_scalar_prefetch=1,
            grid=(steps,),
            in_specs=in_specs,
            out_specs=pl.BlockSpec((hid, tile), lambda i, h: (0, h[0] * steps + i)),
            scratch_shapes=[pltpu.VMEM((slots, tile), jnp.bfloat16)],
        ),
        out_shape=jax.ShapeDtypeStruct((hid, width), jnp.bfloat16),
        input_output_aliases={len(pieces) + 2: 0},
    )(half, *operands)


def matmul_first_kernel(half_ref, *refs):
    matmul_kernel(half_ref, *refs[:-2], None, *refs[-2:])


def matmul_first(half, pieces, ht, width):
    hid, slots = ht.shape
    span = width // 2
    tile = 512
    steps = span // tile
    in_specs = [pl.BlockSpec((p.shape[0], tile), lambda i, h: (0, i)) for p in pieces]
    in_specs.append(pl.BlockSpec((hid, slots), lambda i, h: (0, 0)))
    return pl.pallas_call(
        matmul_first_kernel,
        grid_spec=pltpu.PrefetchScalarGridSpec(
            num_scalar_prefetch=1,
            grid=(steps,),
            in_specs=in_specs,
            out_specs=pl.BlockSpec((hid, tile), lambda i, h: (0, h[0] * steps + i)),
            scratch_shapes=[pltpu.VMEM((slots, tile), jnp.bfloat16)],
        ),
        out_shape=jax.ShapeDtypeStruct((hid, width), jnp.bfloat16),
    )(half, *pieces, ht)


def local(cotangent, slot_token, slot_count, slot_weight, hidden):
    sections, members = lax.axis_size("pipe"), lax.axis_size("dp")
    chips = members // CORES
    me = lax.axis_index("dp")
    chip, core = me // CORES, me % CORES
    first = core == 0
    slots = slot_token.shape[2]
    tokens, width = cotangent.shape[1:]
    units = hidden.shape[3] // members
    span = width // 2

    def ordered(mine, other):
        return jnp.where(first, jnp.concatenate([mine, other]), jnp.concatenate([other, mine]))

    def partner(value):
        return lax.ppermute(value, "dp", [(s, s ^ 1) for s in range(members)])

    def to_chip(value, pairs):
        return lax.ppermute(
            value, "dp", [(a * CORES + i, b * CORES + i) for a, b in pairs for i in range(CORES)]
        )

    def ahead_to(value, flip):
        pairs = [
            (s * members + d, ((s - 1) % sections) * members + (d ^ flip))
            for s in range(sections)
            for d in range(members)
        ]
        return lax.ppermute(value, ("pipe", "dp"), pairs)

    live = (lax.broadcasted_iota(jnp.int32, (slots,), 0) < slot_count[0, 0]).astype(jnp.float32)
    packed = jnp.stack([slot_token[0, 0].astype(jnp.float32), slot_weight[0, 0] * live])
    asked = lax.ppermute(packed, "pipe", [(s, (s + 1) % sections) for s in range(sections)])

    blocks = hidden[0, 0].reshape(slots, chips, CORES, units)
    kept = lax.dynamic_index_in_dim(blocks, core, 2, False)
    given = lax.dynamic_index_in_dim(blocks, 1 - core, 2, False)
    pair_hidden = ordered(kept, partner(given)).transpose(1, 0, 2)
    hidden_parts = [lax.dynamic_index_in_dim(pair_hidden, chip, 0, False)]
    for k in range(1, chips):
        sent = lax.dynamic_index_in_dim(pair_hidden, chip ^ k, 0, False)
        hidden_parts.append(to_chip(sent, [(a, a ^ k) for a in range(chips)]))
    ht = jnp.concatenate(hidden_parts).T

    position = lax.broadcasted_iota(jnp.int32, (slots, tokens), 1)
    chosen = (asked[0].astype(jnp.int32)[:, None] == position).astype(jnp.bfloat16)
    picked = jnp.dot(chosen, cotangent[0], preferred_element_type=jnp.float32)
    rows = (asked[1][:, None] * picked).astype(jnp.bfloat16).reshape(slots, 2, span)
    mine = ahead_to(lax.dynamic_index_in_dim(rows, core, 1, False), 0)
    other = ahead_to(lax.dynamic_index_in_dim(rows, 1 - core, 1, False), 1)
    pair_rows = ordered(mine, other)

    parts = [pair_rows]
    if chips == 4:
        near = to_chip(pair_rows, [(a, a ^ 1) for a in range(chips)])
        far = to_chip(pair_rows, [(a, a ^ 2) for a in range(chips)])
        middle = to_chip(pair_rows, [(1, 2), (2, 1)])
        relayed = to_chip(far, [(1, 0), (2, 3)])
        inner = (chip == 1) | (chip == 2)
        parts += [near, far, jnp.where(inner, middle, relayed)]
    else:
        for k in range(1, chips):
            parts.append(to_chip(pair_rows, [(a, a ^ k) for a in range(chips)]))
    rest = [partner(part) for part in parts]

    out = matmul_first(core.reshape(1), parts, ht, width)
    out = matmul_half((1 - core).reshape(1), rest, ht, out, width)
    return out[None]


def solution(mesh):
    placed = (
        P("pipe", "dp", None),
        P("pipe", "dp", None),
        P("pipe", "dp"),
        P("pipe", "dp", None),
        P("pipe", "dp", None, None),
    )
    return jax.shard_map(
        local, mesh=mesh, in_specs=placed, out_specs=P("pipe", "dp", None), check_vma=False
    )
```

```python
import jax
import jax.numpy as jnp
from jax import lax
from jax.experimental import pallas as pl
from jax.experimental.pallas import tpu as pltpu
from jax.sharding import PartitionSpec as P


CORES = 2
CHUNKS = ((7, True), (5, True))
TILE = 256

VMEM = pl.BlockSpec(memory_space=pltpu.VMEM)
SMEM = pl.BlockSpec(memory_space=pltpu.SMEM)
ANY = pl.BlockSpec(memory_space=pl.ANY)


def live_factors(count, weight):
    def kernel(count_ref, weight_ref, out):
        slot = lax.broadcasted_iota(jnp.int32, weight.shape, 1)
        out[...] = weight_ref[...] * (slot < count_ref[...]).astype(jnp.float32)

    return pl.pallas_call(
        kernel,
        in_specs=[VMEM, VMEM],
        out_specs=VMEM,
        out_shape=jax.ShapeDtypeStruct(weight.shape, weight.dtype),
        compiler_params=pltpu.CompilerParams(vmem_limit_bytes=1 << 20),
        name="live_factors",
    )(count, weight)


def split_hidden(chip, own, chips):
    slots = own.shape[0]
    units = own.shape[1] // chips

    def kernel(chip_ref, own_ref, *outs):
        for k, out in enumerate(outs):
            begin = pl.multiple_of((chip_ref[0] ^ k) * units, 128)
            out[...] = own_ref[:, pl.ds(begin, units)]

    out = jax.ShapeDtypeStruct((slots, units), own.dtype)
    return pl.pallas_call(
        kernel,
        in_specs=[SMEM, VMEM],
        out_specs=[VMEM] * chips,
        out_shape=[out] * chips,
        compiler_params=pltpu.CompilerParams(vmem_limit_bytes=4 << 20),
        name="split_hidden",
    )(chip, own)


def join_hidden(core, kept, got, chips):
    slots = kept.shape[0] // chips

    def kernel(core_ref, kept_ref, got_ref, out):
        for k in range(chips):
            own = kept_ref[k * slots : (k + 1) * slots, :]
            other = got_ref[k * slots : (k + 1) * slots, :]
            begin = 2 * k * slots
            out[begin : begin + slots, :] = jnp.where(core_ref[0] == 0, own, other)
            out[begin + slots : begin + 2 * slots, :] = jnp.where(core_ref[0] == 0, other, own)

    return pl.pallas_call(
        kernel,
        in_specs=[SMEM, VMEM, VMEM],
        out_specs=VMEM,
        out_shape=jax.ShapeDtypeStruct((2 * chips * slots, kept.shape[1]), kept.dtype),
        compiler_params=pltpu.CompilerParams(vmem_limit_bytes=4 << 20),
        name="join_hidden",
    )(core, kept, got)


def product(core, lhs, rows, out, width, half, offset):
    _, units = lhs.shape
    size = rows.shape[1]
    steps = size // TILE
    span = width // 2

    def kernel(core_ref, lhs_ref, rows_ref, *refs):
        out_ref, made, sems = refs[-3:]
        mine = core_ref[0]
        base = (mine if half == 0 else 1 - mine) * span + offset
        copies = []
        for step in range(steps):
            made[step] = lax.dot_general(
                lhs_ref[...],
                rows_ref[:, step * TILE : (step + 1) * TILE],
                (((0,), (0,)), ((), ())),
                preferred_element_type=jnp.float32,
            ).astype(made.dtype)
            begin = pl.multiple_of(base + step * TILE, TILE)
            copy = pltpu.make_async_copy(
                made.at[step], out_ref.at[:, pl.ds(begin, TILE)], sems.at[step]
            )
            copy.start()
            copies.append(copy)
        for copy in copies:
            copy.wait()

    operands = [core, lhs, rows]
    in_specs = [SMEM, VMEM, VMEM]
    aliases = {}
    if out is not None:
        aliases = {len(operands): 0}
        operands.append(out)
        in_specs.append(ANY)
    return pl.pallas_call(
        kernel,
        in_specs=in_specs,
        out_specs=ANY,
        out_shape=jax.ShapeDtypeStruct((units, width), jnp.bfloat16),
        scratch_shapes=[
            pltpu.VMEM((steps, units, TILE), jnp.bfloat16),
            pltpu.SemaphoreType.DMA((steps,)),
        ],
        input_output_aliases=aliases,
        compiler_params=pltpu.CompilerParams(vmem_limit_bytes=10 << 20),
        name="product",
    )(*operands)


def local(cotangent, slot_token, slot_count, slot_weight, hidden):
    sections, members = lax.axis_size("pipe"), lax.axis_size("dp")
    chips = members // CORES
    me = lax.axis_index("dp")
    chip, core = me // CORES, me % CORES
    place = jnp.stack([chip, core]).astype(jnp.int32)
    slots = slot_token.shape[2]
    width = cotangent.shape[2]
    span = width // 2
    first = core == 0

    def partner(value):
        return lax.ppermute(value, "dp", [(s, s ^ 1) for s in range(members)])

    def to_chip(value, pairs):
        return lax.ppermute(
            value, "dp", [(a * CORES + i, b * CORES + i) for a, b in pairs for i in range(CORES)]
        )

    def back_to(value, flip):
        pairs = [
            (s * members + d, ((s - 1) % sections) * members + (d ^ flip))
            for s in range(sections)
            for d in range(members)
        ]
        return lax.ppermute(value, ("pipe", "dp"), pairs)

    def in_order(mine, other):
        return jnp.where(first, jnp.concatenate([mine, other]), jnp.concatenate([other, mine]))

    asked = lax.ppermute(
        slot_token, "pipe", [(s, (s + 1) % sections) for s in range(sections)]
    )
    hidden_parts = list(split_hidden(place[:1], hidden[0, 0], chips))
    for k in range(1, chips):
        hidden_parts[k] = to_chip(hidden_parts[k], [(a, a ^ k) for a in range(chips)])
    came = jnp.concatenate(hidden_parts)
    units = came.shape[1] // CORES
    low, high = came[:, :units], came[:, units:]
    kept, given = jnp.where(first, low, high), jnp.where(first, high, low)
    lhs = join_hidden(place[1:2], kept, partner(given), chips)

    positions = lax.broadcasted_iota(jnp.int32, (slots, cotangent.shape[1]), 1)
    chosen = (asked[0, 0][:, None] == positions).astype(jnp.bfloat16)
    rows = jnp.dot(chosen, cotangent[0], preferred_element_type=jnp.bfloat16)
    factors = live_factors(slot_count, slot_weight[0]).reshape(slots)
    other_factors = partner(factors)
    both = in_order(factors, other_factors)[:, None]

    def at(distance, value):
        return to_chip(value, [(a, a ^ distance) for a in range(chips)])

    out, begin = None, 0
    for share, relayed in CHUNKS:
        end = begin + span * share // sum(part for part, _ in CHUNKS)
        low, high = rows[:, begin:end], rows[:, span + begin : span + end]
        mine = back_to(jnp.where(first, low, high), 0)
        other = back_to(jnp.where(first, high, low), 1)
        pair = (both * in_order(mine, other).astype(jnp.float32)).astype(jnp.bfloat16)
        parts = [pair]
        for k in range(1, chips):
            if relayed and k > 2 and chips == 4:
                parts.append(at(1, parts[2]))
            else:
                parts.append(at(k, pair))
        whole = jnp.concatenate(parts)
        rest = partner(whole)
        out = product(place[1:2], lhs, whole, out, width, 0, begin)
        out = product(place[1:2], lhs, rest, out, width, 1, begin)
        begin = end
    return out[None]


def solution(mesh):
    placed = (
        P("pipe", "dp", None),
        P("pipe", "dp", None),
        P("pipe", "dp"),
        P("pipe", "dp", None),
        P("pipe", "dp", None, None),
    )

    return jax.shard_map(
        local, mesh=mesh, in_specs=placed, out_specs=P("pipe", "dp", None), check_vma=False
    )
```

```python
import jax
import jax.numpy as jnp
from jax import lax
from jax.experimental import pallas as pl
from jax.experimental.pallas import tpu as pltpu
from jax.sharding import PartitionSpec as P


CORES = 2
CHUNKS = ((5, True), (7, True))
CALLS = lambda own, rest: ([own[0], rest[0]], [own[1]], [rest[1]])
TILE = 256

VMEM = pl.BlockSpec(memory_space=pltpu.VMEM)
SMEM = pl.BlockSpec(memory_space=pltpu.SMEM)
ANY = pl.BlockSpec(memory_space=pl.ANY)


def live_factors(count, weight):
    def kernel(count_ref, weight_ref, out):
        slot = lax.broadcasted_iota(jnp.int32, weight.shape, 1)
        out[...] = weight_ref[...] * (slot < count_ref[...]).astype(jnp.float32)

    return pl.pallas_call(
        kernel,
        in_specs=[VMEM, VMEM],
        out_specs=VMEM,
        out_shape=jax.ShapeDtypeStruct(weight.shape, weight.dtype),
        compiler_params=pltpu.CompilerParams(vmem_limit_bytes=1 << 20),
        name="live_factors",
    )(count, weight)


def split_hidden(chip, own, chips):
    slots = own.shape[0]
    units = own.shape[1] // chips

    def kernel(chip_ref, own_ref, *outs):
        for k, out in enumerate(outs):
            begin = pl.multiple_of((chip_ref[0] ^ k) * units, 128)
            out[...] = own_ref[:, pl.ds(begin, units)]

    out = jax.ShapeDtypeStruct((slots, units), own.dtype)
    return pl.pallas_call(
        kernel,
        in_specs=[SMEM, VMEM],
        out_specs=[VMEM] * chips,
        out_shape=[out] * chips,
        compiler_params=pltpu.CompilerParams(vmem_limit_bytes=4 << 20),
        name="split_hidden",
    )(chip, own)


def join_hidden(core, kept, got, chips):
    slots = kept.shape[0] // chips

    def kernel(core_ref, kept_ref, got_ref, out, held):
        for k in range(chips):
            own = kept_ref[k * slots : (k + 1) * slots, :]
            other = got_ref[k * slots : (k + 1) * slots, :]
            begin = 2 * k * slots
            held[begin : begin + slots, :] = jnp.where(core_ref[0] == 0, own, other)
            held[begin + slots : begin + 2 * slots, :] = jnp.where(core_ref[0] == 0, other, own)
        out[...] = held[...].T

    shape = (2 * chips * slots, kept.shape[1])
    return pl.pallas_call(
        kernel,
        in_specs=[SMEM, VMEM, VMEM],
        out_specs=VMEM,
        out_shape=jax.ShapeDtypeStruct(shape[::-1], kept.dtype),
        scratch_shapes=[pltpu.VMEM(shape, kept.dtype)],
        compiler_params=pltpu.CompilerParams(vmem_limit_bytes=4 << 20),
        name="join_hidden",
    )(core, kept, got)


def product(core, lhs, blocks, out, width):
    units = lhs.shape[0]
    span = width // 2
    sizes = [rows.shape[1] // TILE for rows, _, _ in blocks]

    def kernel(core_ref, lhs_ref, *refs):
        out_ref, made, sems = refs[-3:]
        mine = core_ref[0]
        copies = []
        for n, (_, half, offset) in enumerate(blocks):
            base = (mine if half == 0 else 1 - mine) * span + offset
            for step in range(sizes[n]):
                slot = len(copies)
                made[slot] = jnp.dot(
                    lhs_ref[...],
                    refs[n][:, step * TILE : (step + 1) * TILE],
                    preferred_element_type=jnp.float32,
                ).astype(made.dtype)
                begin = pl.multiple_of(base + step * TILE, TILE)
                copy = pltpu.make_async_copy(
                    made.at[slot], out_ref.at[:, pl.ds(begin, TILE)], sems.at[slot]
                )
                copy.start()
                copies.append(copy)
        for copy in copies:
            copy.wait()

    operands = [core, lhs, *(rows for rows, _, _ in blocks)]
    in_specs = [SMEM] + [VMEM] * (len(operands) - 1)
    aliases = {}
    if out is not None:
        aliases = {len(operands): 0}
        operands.append(out)
        in_specs.append(ANY)
    return pl.pallas_call(
        kernel,
        in_specs=in_specs,
        out_specs=ANY,
        out_shape=jax.ShapeDtypeStruct((units, width), jnp.bfloat16),
        scratch_shapes=[
            pltpu.VMEM((sum(sizes), units, TILE), jnp.bfloat16),
            pltpu.SemaphoreType.DMA((sum(sizes),)),
        ],
        input_output_aliases=aliases,
        compiler_params=pltpu.CompilerParams(vmem_limit_bytes=20 << 20),
        name="product",
    )(*operands)


def local(cotangent, slot_token, slot_count, slot_weight, hidden):
    sections, members = lax.axis_size("pipe"), lax.axis_size("dp")
    chips = members // CORES
    me = lax.axis_index("dp")
    chip, core = me // CORES, me % CORES
    place = jnp.stack([chip, core]).astype(jnp.int32)
    slots = slot_token.shape[2]
    width = cotangent.shape[2]
    span = width // 2
    first = core == 0

    def partner(value):
        return lax.ppermute(value, "dp", [(s, s ^ 1) for s in range(members)])

    def to_chip(value, pairs):
        return lax.ppermute(
            value, "dp", [(a * CORES + i, b * CORES + i) for a, b in pairs for i in range(CORES)]
        )

    def at(distance, value):
        return to_chip(value, [(a, a ^ distance) for a in range(chips)])

    def back_to(value, flip):
        pairs = [
            (s * members + d, ((s - 1) % sections) * members + (d ^ flip))
            for s in range(sections)
            for d in range(members)
        ]
        return lax.ppermute(value, ("pipe", "dp"), pairs)

    def in_order(mine, other):
        return jnp.where(first, jnp.concatenate([mine, other]), jnp.concatenate([other, mine]))

    asked = lax.ppermute(
        slot_token, "pipe", [(s, (s + 1) % sections) for s in range(sections)]
    )
    factors = live_factors(slot_count, slot_weight[0]).reshape(slots)
    other_factors = partner(factors)
    both = in_order(factors, other_factors)[:, None]

    hidden_parts = list(split_hidden(place[:1], hidden[0, 0], chips))
    for k in range(1, chips):
        hidden_parts[k] = at(k, hidden_parts[k])
    came = jnp.concatenate(hidden_parts)
    units = came.shape[1] // CORES
    low, high = came[:, :units], came[:, units:]
    kept, given = jnp.where(first, low, high), jnp.where(first, high, low)
    lhs = join_hidden(place[1:2], kept, partner(given), chips)

    positions = lax.broadcasted_iota(jnp.int32, (slots, cotangent.shape[1]), 1)
    chosen = (asked[0, 0][:, None] == positions).astype(jnp.bfloat16)
    rows = jnp.dot(chosen, cotangent[0], preferred_element_type=jnp.bfloat16)

    out, begin, owns, rests = None, 0, [], []
    for share, relayed in CHUNKS:
        end = begin + span * share // sum(part for part, _ in CHUNKS)
        low, high = rows[:, begin:end], rows[:, span + begin : span + end]
        mine = back_to(jnp.where(first, low, high), 0)
        other = back_to(jnp.where(first, high, low), 1)
        pair = (both * in_order(mine, other).astype(jnp.float32)).astype(jnp.bfloat16)
        parts = [pair]
        for k in range(1, chips):
            if relayed and k > 2 and chips == 4:
                carried = jnp.where(chip < chips, parts[2], pair)
                parts.append(at(1, carried))
            else:
                parts.append(at(k, pair))
        whole = jnp.concatenate(parts)
        rest = partner(whole)
        owns.append((whole, 0, begin))
        rests.append((rest, 1, begin))
        begin = end
    for blocks in CALLS(owns, rests):
        out = product(place[1:2], lhs, blocks, out, width)
    return out[None]


def solution(mesh):
    placed = (
        P("pipe", "dp", None),
        P("pipe", "dp", None),
        P("pipe", "dp"),
        P("pipe", "dp", None),
        P("pipe", "dp", None, None),
    )

    return jax.shard_map(
        local, mesh=mesh, in_specs=placed, out_specs=P("pipe", "dp", None), check_vma=False
    )
```

```python
import jax
import jax.numpy as jnp
from jax import lax
from jax.experimental import pallas as pl
from jax.experimental.pallas import tpu as pltpu
from jax.sharding import PartitionSpec as P


CORES = 2
CHUNKS = ((11, True), (13, True))
CALLS = lambda own, rest: ([own[0]], [rest[0]], [own[1]], [rest[1]])
TILE = 256

VMEM = pl.BlockSpec(memory_space=pltpu.VMEM)
SMEM = pl.BlockSpec(memory_space=pltpu.SMEM)
ANY = pl.BlockSpec(memory_space=pl.ANY)


def live_factors(count, weight):
    def kernel(count_ref, weight_ref, out):
        slot = lax.broadcasted_iota(jnp.int32, weight.shape, 1)
        out[...] = weight_ref[...] * (slot < count_ref[...]).astype(jnp.float32)

    return pl.pallas_call(
        kernel,
        in_specs=[VMEM, VMEM],
        out_specs=VMEM,
        out_shape=jax.ShapeDtypeStruct(weight.shape, weight.dtype),
        compiler_params=pltpu.CompilerParams(vmem_limit_bytes=1 << 20),
        name="live_factors",
    )(count, weight)


def split_hidden(chip, own, chips):
    slots = own.shape[0]
    units = own.shape[1] // chips

    def kernel(chip_ref, own_ref, *outs):
        for k, out in enumerate(outs):
            begin = pl.multiple_of((chip_ref[0] ^ k) * units, 128)
            out[...] = own_ref[:, pl.ds(begin, units)]

    out = jax.ShapeDtypeStruct((slots, units), own.dtype)
    return pl.pallas_call(
        kernel,
        in_specs=[SMEM, VMEM],
        out_specs=[VMEM] * chips,
        out_shape=[out] * chips,
        compiler_params=pltpu.CompilerParams(vmem_limit_bytes=4 << 20),
        name="split_hidden",
    )(chip, own)


def join_hidden(core, kept, got, chips):
    slots = kept.shape[0] // chips

    def kernel(core_ref, kept_ref, got_ref, out, held):
        for k in range(chips):
            own = kept_ref[k * slots : (k + 1) * slots, :]
            other = got_ref[k * slots : (k + 1) * slots, :]
            begin = 2 * k * slots
            held[begin : begin + slots, :] = jnp.where(core_ref[0] == 0, own, other)
            held[begin + slots : begin + 2 * slots, :] = jnp.where(core_ref[0] == 0, other, own)
        out[...] = held[...].T

    shape = (2 * chips * slots, kept.shape[1])
    return pl.pallas_call(
        kernel,
        in_specs=[SMEM, VMEM, VMEM],
        out_specs=VMEM,
        out_shape=jax.ShapeDtypeStruct(shape[::-1], kept.dtype),
        scratch_shapes=[pltpu.VMEM(shape, kept.dtype)],
        compiler_params=pltpu.CompilerParams(vmem_limit_bytes=4 << 20),
        name="join_hidden",
    )(core, kept, got)


def product(core, lhs, blocks, out, width):
    units = lhs.shape[0]
    span = width // 2
    steps = [
        (n, half, offset, at, min(TILE, rows.shape[1] - at))
        for n, (rows, half, offset) in enumerate(blocks)
        for at in range(0, rows.shape[1], TILE)
    ]

    def kernel(core_ref, lhs_ref, *refs):
        out_ref, made, sems = refs[-3:]
        mine = core_ref[0]
        copies = []
        for slot, (n, half, offset, at, size) in enumerate(steps):
            made[slot, :, :size] = jnp.dot(
                lhs_ref[...],
                refs[n][:, at : at + size],
                preferred_element_type=jnp.float32,
            ).astype(made.dtype)
            begin = (mine if half == 0 else 1 - mine) * span + offset + at
            copies.append(
                pltpu.make_async_copy(
                    made.at[slot, :, pl.ds(0, size)],
                    out_ref.at[:, pl.ds(pl.multiple_of(begin, 128), size)],
                    sems.at[slot],
                )
            )
            copies[-1].start()
        for copy in copies:
            copy.wait()

    operands = [core, lhs, *(rows for rows, _, _ in blocks)]
    in_specs = [SMEM] + [VMEM] * (len(operands) - 1)
    aliases = {}
    if out is not None:
        aliases = {len(operands): 0}
        operands.append(out)
        in_specs.append(ANY)
    return pl.pallas_call(
        kernel,
        in_specs=in_specs,
        out_specs=ANY,
        out_shape=jax.ShapeDtypeStruct((units, width), jnp.bfloat16),
        scratch_shapes=[
            pltpu.VMEM((len(steps), units, TILE), jnp.bfloat16),
            pltpu.SemaphoreType.DMA((len(steps),)),
        ],
        input_output_aliases=aliases,
        compiler_params=pltpu.CompilerParams(vmem_limit_bytes=20 << 20),
        name="product",
    )(*operands)


def local(cotangent, slot_token, slot_count, slot_weight, hidden):
    sections, members = lax.axis_size("pipe"), lax.axis_size("dp")
    chips = members // CORES
    me = lax.axis_index("dp")
    chip, core = me // CORES, me % CORES
    place = jnp.stack([chip, core]).astype(jnp.int32)
    slots = slot_token.shape[2]
    width = cotangent.shape[2]
    span = width // 2
    first = core == 0

    def partner(value):
        return lax.ppermute(value, "dp", [(s, s ^ 1) for s in range(members)])

    def to_chip(value, pairs):
        return lax.ppermute(
            value, "dp", [(a * CORES + i, b * CORES + i) for a, b in pairs for i in range(CORES)]
        )

    def at(distance, value):
        return to_chip(value, [(a, a ^ distance) for a in range(chips)])

    def back_to(value, flip):
        pairs = [
            (s * members + d, ((s - 1) % sections) * members + (d ^ flip))
            for s in range(sections)
            for d in range(members)
        ]
        return lax.ppermute(value, ("pipe", "dp"), pairs)

    def in_order(mine, other):
        return jnp.where(first, jnp.concatenate([mine, other]), jnp.concatenate([other, mine]))

    asked = lax.ppermute(
        slot_token, "pipe", [(s, (s + 1) % sections) for s in range(sections)]
    )
    factors = live_factors(slot_count, slot_weight[0]).reshape(slots)
    other_factors = partner(factors)
    both = in_order(factors, other_factors)[:, None]

    hidden_parts = list(split_hidden(place[:1], hidden[0, 0], chips))
    for k in range(1, chips):
        hidden_parts[k] = at(k, hidden_parts[k])
    came = jnp.concatenate(hidden_parts)
    units = came.shape[1] // CORES
    low, high = came[:, :units], came[:, units:]
    kept, given = jnp.where(first, low, high), jnp.where(first, high, low)
    lhs = join_hidden(place[1:2], kept, partner(given), chips)

    positions = lax.broadcasted_iota(jnp.int32, (slots, cotangent.shape[1]), 1)
    chosen = (asked[0, 0][:, None] == positions).astype(jnp.bfloat16)
    rows = jnp.dot(chosen, cotangent[0], preferred_element_type=jnp.bfloat16)

    out, begin, owns, rests = None, 0, [], []
    for share, relayed in CHUNKS:
        end = begin + span * share // sum(part for part, _ in CHUNKS)
        low, high = rows[:, begin:end], rows[:, span + begin : span + end]
        mine = back_to(jnp.where(first, low, high), 0)
        other = back_to(jnp.where(first, high, low), 1)
        pair = (both * in_order(mine, other).astype(jnp.float32)).astype(jnp.bfloat16)
        parts = [pair]
        for k in range(1, chips):
            if relayed and k > 2 and chips == 4:
                carried = jnp.where(chip < chips, parts[2], pair)
                parts.append(at(1, carried))
            else:
                parts.append(at(k, pair))
        whole = jnp.concatenate(parts)
        rest = partner(whole)
        owns.append((whole, 0, begin))
        rests.append((rest, 1, begin))
        begin = end
    for blocks in CALLS(owns, rests):
        out = product(place[1:2], lhs, blocks, out, width)
    return out[None]


def solution(mesh):
    placed = (
        P("pipe", "dp", None),
        P("pipe", "dp", None),
        P("pipe", "dp"),
        P("pipe", "dp", None),
        P("pipe", "dp", None, None),
    )

    return jax.shard_map(
        local, mesh=mesh, in_specs=placed, out_specs=P("pipe", "dp", None), check_vma=False
    )
```
